256 devices in a mesh: group: 2 (over x_hi), gz: 128 (over x_lo, y, z, core).
Axes of the slice: x: 4 (x_hi: 2, x_lo: 2; x = x_hi * 2 + x_lo), y: 4, z: 8, core: 2. Of those that a mesh axis runs over, the one named last changes fastest.
Arguments:
- velocity: float32 [2, 3, 256, 256, 256], P('group', None, 'gz'), may hold values from -5 to 5
- fringe_start: int32 [1], replicated, may hold values from 0 to 224
- turbine_level: int32 [64], replicated, may hold values from 0 to 255
- turbine_row: int32 [64], replicated, may hold values from 0 to 255
- turbine_col: int32 [64], replicated, may hold values from 0 to 255
- thrust: float32 [64], replicated, may hold values from 1 to 12
- green_basis: float32 [256, 256], replicated, may hold values from -0.5 to 2.5
- eigen_shift: float32 [256], replicated, may hold values from 0.05 to 1
Outputs:
- updated: float32 [2, 3, 256, 256, 256], P('group', None, 'gz')
- pressure: float32 [2, 256, 256, 256], P('group', 'gz')
The draws below stay inside these ranges and needn't reach their ends.
All inputs are finite; a program needn't handle non-finite values.
Results may differ from the reference program's by a relative error of at most 0.00011.
Values sent between devices are 32-bit elements; how exact they have to be, the bound alone decides.
No kernel may reach another device: no remote copies, remote signals or barrier semaphores. Data moves between devices by JAX's collectives and lax.ppermute only.
A program may use at most 64 MiB of HBM per device.

```python
import math
import jax
import jax.numpy as jnp
from jax import lax

NY = 256
NX = 256
TURB = 64
FRINGE = 32
NZ = 256
MEMBERS = 2


def draw_green_basis(key, part):
    noise = jax.random.normal(jax.random.fold_in(key, 7), (NZ, NZ), jnp.float32) * (0.8 / math.sqrt(NZ))
    noise = jnp.clip(noise, -0.5, 0.5)
    leading = 2.0
    return leading * jnp.eye(NZ, dtype=jnp.float32) + noise


def with_ends(result, rng, least, high):
    index_at = [jax.random.randint(jax.random.fold_in(rng, axis), (), 0, length) for axis, length in enumerate(result.shape)]
    widest = result.shape.index(max(result.shape))
    beside = index_at[:widest] + [(index_at[widest] + 1) % result.shape[widest]] + index_at[widest + 1:]
    return result.at[tuple(index_at)].set(least).at[tuple(beside)].set(high)


def steps_of(own_key, dims, split, low, top_value):
    def one(position, shards_of):
        heights = jax.random.uniform(jax.random.fold_in(jax.random.fold_in(own_key, 6), position), (shards_of,), jnp.float32, low / len(split), top_value / len(split))
        return jnp.repeat(jnp.exp(heights), dims[position] // shards_of).reshape((-1,) + (1,) * (len(dims) - position - 1))

    loudness = one(*split[0])
    for cut in split[1:]:
        loudness = loudness * one(*cut)
    return loudness


def gaussian(key, dims, spread, most, shards=(), kind=jnp.bfloat16):
    values = jax.random.normal(key, dims, jnp.float32) * spread
    if len(shards) > 0:
        values = steps_of(key, dims, shards, -0.22, 0.18) * values
    return jnp.clip(values, min=-most, max=most).astype(kind)


def setup_inputs(seed: int = 0) -> dict:
    key_of = jax.random.split(jax.random.key(seed), 9)
    return {
        "velocity": gaussian(key_of[0], (MEMBERS, 3, NZ, NY, NX), 1.0, 5.0, ((0, 2), (2, 128)), jnp.float32),
        "fringe_start": jax.random.randint(key_of[1], (1,), 0, NX - FRINGE + 1).astype(jnp.int32),
        "turbine_level": with_ends(jax.random.randint(key_of[2], (TURB,), 0, NZ), jax.random.fold_in(key_of[2], 1), 0, NZ - 1).astype(jnp.int32),
        "turbine_row": with_ends(jax.random.randint(key_of[3], (TURB,), 0, NY), jax.random.fold_in(key_of[3], 1), 0, NY - 1).astype(jnp.int32),
        "turbine_col": with_ends(jax.random.randint(key_of[4], (TURB,), 0, NX), jax.random.fold_in(key_of[4], 1), 0, NX - 1).astype(jnp.int32),
        "thrust": jnp.clip(jnp.exp(jax.random.uniform(key_of[5], (TURB,), jnp.float32, math.log(1.0), math.log(12.0))), 1.0, 12.0),
        "green_basis": draw_green_basis(jax.random.fold_in(key_of[8], 71), 0),
        "eigen_shift": jnp.clip(jnp.exp(jax.random.uniform(key_of[7], (NZ,), jnp.float32, math.log(0.05), math.log(1.0))), 0.05, 1.0),
    }


highest = lax.Precision.HIGHEST
time_step = 0.25

def wavenumber(ids, length):
    middle = length // 2
    return jnp.where(ids <= middle, ids, ids - middle)

def real_basis(length):
    row_ids = jnp.arange(length, dtype=jnp.int32)[:, None]
    col_ids = jnp.arange(length, dtype=jnp.int32)[None, :]
    middle = length // 2
    phases = 2.0 * jnp.pi / length * (wavenumber(row_ids, length) * col_ids % length).astype(jnp.float32)
    edges = (row_ids == 0) | (row_ids == middle)
    weights_norm = jnp.sqrt(jnp.where(edges, 1.0, 2.0) / length)
    return (jnp.where(row_ids <= middle, jnp.cos(phases), jnp.sin(phases)) * weights_norm).astype(jnp.float32)

def derivative(length):
    row_ids = jnp.arange(length, dtype=jnp.int32)[:, None]
    col_ids = jnp.arange(length, dtype=jnp.int32)[None, :]
    middle = length // 2
    omega_upper = 2.0 * jnp.pi / length * row_ids.astype(jnp.float32)
    omega_lower = 2.0 * jnp.pi / length * (row_ids - middle).astype(jnp.float32)
    upper = jnp.where((row_ids >= 1) & (row_ids < middle) & (col_ids == row_ids + middle), omega_upper, 0.0)
    lower = jnp.where((row_ids > middle) & (col_ids == row_ids - middle), -omega_lower, 0.0)
    basis = real_basis(length)
    return jnp.dot(basis.T, jnp.dot(upper + lower, basis, precision=highest), precision=highest)

def wave_square(ids, length):
    wave = wavenumber(ids, length).astype(jnp.float32) * (2.0 * jnp.pi / length)
    return wave * wave

def x_derivative(field, matrix):
    return jnp.einsum('...yb,ab->...ya', field, matrix, precision=highest)

def y_derivative(field, matrix):
    return jnp.einsum('ab,...bx->...ax', matrix, field, precision=highest)

def forward_plane(field, basis_y, basis_x):
    return x_derivative(y_derivative(field, basis_y), basis_x)

def inverse_plane(field, basis_y, basis_x):
    return x_derivative(y_derivative(field, basis_y.T), basis_x.T)

def advection(fields, vertical, deriv_y, deriv_x):
    along_x = x_derivative(fields, deriv_x)
    along_y = y_derivative(fields, deriv_y)
    return -(fields[0:1] * along_x + fields[1:2] * along_y + fields[2:3] * vertical)

def fringe_shape(offset):
    sine_part = jnp.sin(jnp.pi * (offset + 0.5) / FRINGE)
    return sine_part * sine_part

def reference(velocity, fringe_start, turbine_level, turbine_row, turbine_col, thrust, green_basis, eigen_shift):
    basis_y = real_basis(NY)
    basis_x = real_basis(NX)
    deriv_y = derivative(NY)
    deriv_x = derivative(NX)
    modes_ksq = (wave_square(jnp.arange(NY, dtype=jnp.int32)[:, None], NY) + wave_square(jnp.arange(NX, dtype=jnp.int32)[None, :], NX)).reshape(NY * NX)
    offset = jnp.arange(NX, dtype=jnp.int32) - fringe_start[0]
    inside = (offset >= 0) & (offset < FRINGE)
    fringe_ramp = jnp.where(inside, fringe_shape(offset.astype(jnp.float32)), 0.0)
    results = []
    pressures = []
    for member in range(MEMBERS):
        fields = velocity[member]
        is_farm = 1.0 if member > 0 else 0.0
        padded = jnp.pad(fields, ((0, 0), (1, 1), (0, 0), (0, 0)))
        vertical = 0.5 * (padded[:, 2:] - padded[:, :-2])
        tendency = advection(fields, vertical, deriv_y, deriv_x)
        speed = fields[0]
        cell_speed = speed[turbine_level, turbine_row, turbine_col]
        drag_force = -thrust * jnp.abs(cell_speed) * cell_speed
        placed = jnp.zeros_like(speed).at[turbine_level, turbine_row, turbine_col].add(drag_force)
        tendency = jnp.concatenate([tendency[0:1] + is_farm * placed[None], tendency[1:]], 0)
        predicted = fields + time_step * tendency
        horizontal = predicted[:2] + is_farm * fringe_ramp * (velocity[0, :2] - predicted[:2])
        upward = predicted[2]
        below = jnp.concatenate([jnp.zeros((1, NY, NX), jnp.float32), upward[:-1]], 0)
        divergence = x_derivative(horizontal[0], deriv_x) + y_derivative(horizontal[1], deriv_y) + (upward - below)
        spectrum = forward_plane(divergence, basis_y, basis_x).reshape(NZ, NY * NX)
        scaled = jnp.dot(green_basis, spectrum, precision=highest) / (eigen_shift[:, None] + modes_ksq[None, :])
        pressure_modes = jnp.dot(green_basis.T, scaled, precision=highest)
        rise_modes = jnp.concatenate([pressure_modes[1:], jnp.zeros((1, NY * NX), jnp.float32)], 0) - pressure_modes
        pressure = inverse_plane(pressure_modes.reshape(NZ, NY, NX), basis_y, basis_x)
        rise = inverse_plane(rise_modes.reshape(NZ, NY, NX), basis_y, basis_x)
        correction = jnp.stack([x_derivative(pressure, deriv_x), y_derivative(pressure, deriv_y), rise], 0)
        results.append(jnp.concatenate([horizontal, upward[None]], 0) - correction)
        pressures.append(pressure)
    return (jnp.stack(results, 0), jnp.stack(pressures, 0))
```

```python
import numpy as np
import jax
import jax.numpy as jnp
from jax import lax
from jax.experimental import pallas as pl
from jax.experimental.pallas import tpu as pltpu
from jax.sharding import PartitionSpec as P

FRINGE = 32
N = 256
MID = N // 2
LANES = 128
STEP = 0.25
HALF = 0.5 * STEP
F32 = jnp.float32
BF16 = jnp.bfloat16


def wave_numbers():
    ids = np.arange(N)
    return np.where(ids <= MID, ids, ids - MID)


def basis_table():
    ids = np.arange(N)
    wave = wave_numbers()
    phases = 2.0 * np.pi / N * ((wave[:, None] * ids[None, :]) % N)
    edges = (ids == 0) | (ids == MID)
    norm = np.sqrt(np.where(edges, 1.0, 2.0) / N)[:, None]
    return np.where(ids[:, None] <= MID, np.cos(phases), np.sin(phases)) * norm


def derivative_table():
    basis = basis_table()
    coupling = np.zeros((N, N))
    for j in range(1, MID):
        coupling[j, j + MID] = 2.0 * np.pi * j / N
        coupling[j + MID, j] = -2.0 * np.pi * j / N
    return basis.T @ coupling @ basis


def halves(table):
    table = np.asarray(table, np.float32)
    high = table.astype(BF16)
    low = (table - high.astype(np.float32)).astype(BF16)
    return np.stack([high, low])


def ramp_row():
    offset = np.arange(FRINGE)
    row = np.zeros((8, N), np.float32)
    row[:, :FRINGE] = np.sin(np.pi * (offset + 0.5) / FRINGE) ** 2
    return row


def split(value):
    high = value.astype(BF16)
    low = (value - high.astype(F32)).astype(BF16)
    return high, low


def dot(a, b):
    return jnp.dot(a, b, preferred_element_type=F32)


def times(value, table):
    high, low = split(value)
    return dot(high, table[1]) + dot(low, table[0]) + dot(high, table[0])


def after(table, value):
    high, low = split(value)
    return dot(table[1], high) + dot(table[0], low) + dot(table[0], high)


def pack_kernel(info, horizontal, window):
    start = info[0]
    lane = lax.broadcasted_iota(jnp.int32, (64, LANES), 1)
    for plane in range(4):
        packed = jnp.zeros((64, LANES), F32)
        for part in range(4):
            rows = horizontal[plane // 2, plane % 2, part * 64 : part * 64 + 64, :]
            shift = lax.rem(32 * part - start + N, N)
            rolled = pltpu.roll(rows, shift, 1)[:, :LANES]
            inside = (lane >= 32 * part) & (lane < 32 * part + 32)
            packed = jnp.where(inside, rolled, packed)
        window[plane * 64 : plane * 64 + 64, :] = packed


def local_kernel(
    info, level, row, col, thrust, fields, deriv, green, eigen, partial, green_halves, inverse
):
    table = (deriv[0], deriv[1])
    for at in range(2):
        u = fields[0, at]
        v = fields[1, at]
        w = fields[2, at]
        for comp in range(3):
            here = fields[comp, at]
            along_x = -times(here, table)
            along_y = after(table, here)
            other = fields[comp, 1 - at]
            vertical = w * other if at == 0 else -(w * other)
            partial[comp, at] = here - STEP * (u * along_x + v * along_y) - HALF * vertical

    is_farm = info[2]
    first_level = info[1] * 2
    lane = lax.broadcasted_iota(jnp.int32, (1, N), 1)

    def place(turbine, carry):
        at = level[turbine] - first_level

        @pl.when((at >= 0) & (at < 2) & (is_farm > 0))
        def _():
            where_row = row[turbine]
            speed = fields[0, at, pl.ds(where_row, 1), :]
            drag = -thrust[turbine] * jnp.abs(speed) * speed
            old = partial[0, at, pl.ds(where_row, 1), :]
            partial[0, at, pl.ds(where_row, 1), :] = old + jnp.where(
                lane == col[turbine], STEP * drag, 0.0
            )

        return carry

    lax.fori_loop(0, level.shape[0], place, 0)

    basis = green[...]
    high, low = split(basis)
    green_halves[0] = high
    green_halves[1] = low
    high, low = split(basis.T)
    green_halves[2] = high
    green_halves[3] = low

    owner = info[1]
    tile = owner // 2
    lanes = lax.broadcasted_iota(jnp.int32, (8, LANES), 1) + LANES * (tile % 2)
    wave_x = jnp.where(lanes <= MID, lanes, lanes - MID).astype(F32) * (2.0 * np.pi / N)
    for part in range(4):
        ky = 8 * (tile // 2) + 4 * (owner % 2) + part
        rows = jnp.zeros((8, LANES), jnp.int32) + ky
        wave_y = jnp.where(rows <= MID, rows, rows - MID).astype(F32) * (2.0 * np.pi / N)
        square = (wave_y * wave_y + wave_x * wave_x)[0:1]
        inverse[part] = 1.0 / (eigen[...] + square)


def forward_kernel(
    info, w_own, partial, below, above, window, deriv, basis, basis_t, ramp, predicted, sent
):
    table = (deriv[0], deriv[1])
    start = info[0]
    w_low = w_own[0]
    w_high = w_own[1]
    shape = pltpu.roll(ramp[...], start, 1)[0:1]
    shape = shape * info[2].astype(F32)
    lane_zero = jnp.zeros((64, LANES), F32)
    for comp in range(3):
        for at in range(2):
            if at == 0:
                value = partial[comp, 0] + HALF * (w_low * below[comp])
            else:
                value = partial[comp, 1] - HALF * (w_high * above[comp])
            if comp < 2:
                plane = comp * 2 + at
                pieces = []
                for part in range(4):
                    block = window[plane * 64 : plane * 64 + 64, :]
                    wide = jnp.concatenate([block, lane_zero], axis=1)
                    shift = lax.rem(start - 32 * part + N, N)
                    pieces.append(pltpu.roll(wide, shift, 1))
                inflow = jnp.concatenate(pieces, axis=0)
                value = value + shape * (inflow - value)
            predicted[comp, at] = value
    w_ghost = below[2]
    ghost = w_ghost - STEP * (
        below[1] * after(table, w_ghost) - below[0] * times(w_ghost, table)
    )
    ghost = ghost - HALF * (w_ghost * (w_low - below[3]))
    under = ghost
    for at in range(2):
        upward = predicted[2, at]
        divergence = (
            after(table, predicted[1, at]) - times(predicted[0, at], table) + (upward - under)
        )
        under = upward
        spectrum = times(after((basis[0], basis[1]), divergence), (basis_t[0], basis_t[1]))
        for tile in range(64):
            r = 8 * (tile // 2)
            c = LANES * (tile % 2)
            block = spectrum[r : r + 8, c : c + LANES]
            sent[2 * tile, 4 * at : 4 * at + 4, :] = block[0:4]
            sent[2 * tile + 1, 4 * at : 4 * at + 4, :] = block[4:8]


def column_kernel(modes, green_halves, inverse, out):
    for part in range(4):
        rows = pl.ds(part, N, stride=4)
        scaled = after((green_halves[0], green_halves[1]), modes[rows, :]) * inverse[part]
        out[rows, :] = after((green_halves[2], green_halves[3]), scaled)


def unpack(planes, at):
    columns = []
    for side in range(2):
        rows = []
        for block in range(32):
            tile = 2 * block + side
            rows.append(planes[2 * tile, 4 * at : 4 * at + 4, :])
            rows.append(planes[2 * tile + 1, 4 * at : 4 * at + 4, :])
        columns.append(jnp.concatenate(rows, axis=0))
    return jnp.concatenate(columns, axis=1)


def lowest_kernel(planes, basis, basis_t, lowest):
    modes = unpack(planes, 0)
    lowest[...] = times(after((basis_t[0], basis_t[1]), modes), (basis[0], basis[1]))


def correct_kernel(planes, lowest, predicted, deriv, basis, basis_t, updated, pressure):
    table = (deriv[0], deriv[1])
    low = lowest[...]
    modes = unpack(planes, 1)
    high = times(after((basis_t[0], basis_t[1]), modes), (basis[0], basis[1]))
    pressure[0, 0] = low
    pressure[0, 1] = high
    for at, value in enumerate((low, high)):
        updated[0, 0, at] = predicted[0, at] + times(value, table)
        updated[0, 1, at] = predicted[1, at] - after(table, value)
    updated[0, 2, 0] = predicted[2, 0] - (high - low)
    updated[0, 2, 1] = predicted[2, 1] + high


def call(kernel, outs, args, scalars=0, limit=24 << 20, **kwargs):
    smem = pl.BlockSpec(memory_space=pltpu.SMEM)
    vmem = pl.BlockSpec(memory_space=pltpu.VMEM)
    in_specs = [smem] * scalars + [vmem] * (len(args) - scalars)
    return pl.pallas_call(
        kernel,
        out_shape=outs,
        in_specs=in_specs,
        out_specs=jax.tree.map(lambda _: vmem, outs),
        compiler_params=pltpu.CompilerParams(vmem_limit_bytes=limit),
        **kwargs,
    )(*args)


def shaped(*dims, dtype=F32):
    return jax.ShapeDtypeStruct(dims, dtype)


def local(
    velocity,
    fringe_start,
    turbine_level,
    turbine_row,
    turbine_col,
    thrust,
    green_basis,
    eigen_shift,
):
    fields = velocity[0]
    count = lax.axis_size("gz")
    deriv = jnp.asarray(halves(derivative_table()))
    basis = jnp.asarray(halves(basis_table()))
    basis_t = jnp.asarray(halves(basis_table().T))
    ramp = jnp.asarray(ramp_row())
    slab_id = lax.axis_index("gz").astype(jnp.int32)
    group_id = lax.axis_index("group").astype(jnp.int32)
    info = jnp.concatenate([fringe_start, slab_id[None], group_id[None]])

    rising = jnp.concatenate([fields[:, 1], fields[2:3, 0]], 0)
    below = lax.ppermute(rising, "gz", [(i, i + 1) for i in range(count - 1)])
    above = lax.ppermute(fields[:, 0], "gz", [(i + 1, i) for i in range(count - 1)])
    window = call(pack_kernel, shaped(4 * 64, LANES), (info, fields[:2]), scalars=1)
    window = lax.ppermute(window, "group", [(0, 1)])

    eigen = jnp.broadcast_to(eigen_shift[:, None], (N, LANES))
    partial, green_halves, inverse = call(
        local_kernel,
        (shaped(3, 2, N, N), shaped(4, N, N, dtype=BF16), shaped(4, N, LANES)),
        (
            info,
            turbine_level,
            turbine_row,
            turbine_col,
            thrust,
            fields,
            deriv,
            green_basis,
            eigen,
        ),
        scalars=5,
    )
    predicted, sent = call(
        forward_kernel,
        (shaped(3, 2, N, N), shaped(count, 8, LANES)),
        (info, fields[2], partial, below, above, window, deriv, basis, basis_t, ramp),
        scalars=1,
    )
    modes = lax.all_to_all(sent, "gz", split_axis=0, concat_axis=0, tiled=True)
    solved = call(
        column_kernel,
        shaped(count * 8, LANES),
        (modes.reshape(count * 8, LANES), green_halves, inverse),
    )
    planes = lax.all_to_all(
        solved.reshape(count, 8, LANES), "gz", split_axis=0, concat_axis=0, tiled=True
    )
    lowest = call(lowest_kernel, shaped(N, N), (planes, basis, basis_t))
    higher = lax.ppermute(lowest, "gz", [(i + 1, i) for i in range(count - 1)])
    updated, pressure = call(
        correct_kernel,
        (shaped(1, 3, 2, N, N), shaped(1, 2, N, N)),
        (planes, lowest, predicted, deriv, basis, basis_t),
    )
    last = updated[:, 2:3, 1:2] - higher[None, None, None]
    updated = lax.dynamic_update_slice(updated, last, (0, 2, 1, 0, 0))
    return (updated, pressure)


def solution(mesh):
    return jax.shard_map(
        local,
        mesh=mesh,
        in_specs=(P("group", None, "gz", None, None), P(), P(), P(), P(), P(), P(), P()),
        out_specs=(P("group", None, "gz", None, None), P("group", "gz", None, None)),
        check_vma=False,
    )
```

```python
import numpy as np
import jax
import jax.numpy as jnp
from jax import lax
from jax.experimental import pallas as pl
from jax.experimental.pallas import tpu as pltpu
from jax.sharding import PartitionSpec as P

FRINGE = 32
N = 256
MID = N // 2
LANES = 128
STEP = 0.25
HALF = 0.5 * STEP
F32 = jnp.float32
BF16 = jnp.bfloat16


def wave_numbers():
    ids = np.arange(N)
    return np.where(ids <= MID, ids, ids - MID)


def basis_table():
    ids = np.arange(N)
    wave = wave_numbers()
    phases = 2.0 * np.pi / N * ((wave[:, None] * ids[None, :]) % N)
    edges = (ids == 0) | (ids == MID)
    norm = np.sqrt(np.where(edges, 1.0, 2.0) / N)[:, None]
    return np.where(ids[:, None] <= MID, np.cos(phases), np.sin(phases)) * norm


def derivative_table():
    basis = basis_table()
    coupling = np.zeros((N, N))
    for j in range(1, MID):
        coupling[j, j + MID] = 2.0 * np.pi * j / N
        coupling[j + MID, j] = -2.0 * np.pi * j / N
    return basis.T @ coupling @ basis


def halves(table):
    table = np.asarray(table, np.float32)
    high = table.astype(BF16)
    low = (table - high.astype(np.float32)).astype(BF16)
    return np.stack([high, low])


def ramp_row():
    offset = np.arange(FRINGE)
    row = np.zeros((8, N), np.float32)
    row[:, :FRINGE] = np.sin(np.pi * (offset + 0.5) / FRINGE) ** 2
    return row


def split(value):
    high = value.astype(BF16)
    low = (value - high.astype(F32)).astype(BF16)
    return high, low


def dot(a, b):
    return jnp.dot(a, b, preferred_element_type=F32)


def times(value, table):
    high, low = split(value)
    return dot(high, table[1]) + dot(low, table[0]) + dot(high, table[0])


def after(table, value):
    high, low = split(value)
    return dot(table[1], high) + dot(table[0], low) + dot(table[0], high)


def edges_kernel(fields, rising, falling, rising_flat, sems):
    moves = (
        (fields.at[2, 1], rising.at[0]),
        (fields.at[2, 0], rising.at[1]),
        (fields.at[:, 0], falling),
        (fields.at[pl.ds(0, 2), 1], rising_flat),
    )
    copies = [
        pltpu.make_async_copy(source, target, sems.at[i])
        for i, (source, target) in enumerate(moves)
    ]
    for copy in copies:
        copy.start()
    for copy in copies:
        copy.wait()


def pack_kernel(info, fields, window):
    start = info[0]
    lane = lax.broadcasted_iota(jnp.int32, (64, LANES), 1)
    for plane in range(4):
        packed = jnp.zeros((64, LANES), F32)
        for part in range(4):
            rows = fields[plane // 2, plane % 2, part * 64 : part * 64 + 64, :]
            shift = lax.rem(32 * part - start + N, N)
            rolled = pltpu.roll(rows, shift, 1)[:, :LANES]
            inside = (lane >= 32 * part) & (lane < 32 * part + 32)
            packed = jnp.where(inside, rolled, packed)
        window[plane * 64 : plane * 64 + 64, :] = packed


def local_kernel(
    info, level, row, col, thrust, fields, deriv, green, eigen, partial, green_halves, inverse
):
    table = (deriv[0], deriv[1])
    for at in range(2):
        u = fields[0, at]
        v = fields[1, at]
        w = fields[2, at]
        for comp in range(3):
            here = fields[comp, at]
            along_x = -times(here, table)
            along_y = after(table, here)
            other = fields[comp, 1 - at]
            vertical = w * other if at == 0 else -(w * other)
            partial[comp, at] = here - STEP * (u * along_x + v * along_y) - HALF * vertical

    is_farm = info[2]
    first_level = info[1] * 2
    lane = lax.broadcasted_iota(jnp.int32, (1, N), 1)

    def place(turbine, carry):
        at = level[turbine] - first_level

        @pl.when((at >= 0) & (at < 2) & (is_farm > 0))
        def _():
            where_row = row[turbine]
            speed = fields[0, at, pl.ds(where_row, 1), :]
            drag = -thrust[turbine] * jnp.abs(speed) * speed
            old = partial[0, at, pl.ds(where_row, 1), :]
            partial[0, at, pl.ds(where_row, 1), :] = old + jnp.where(
                lane == col[turbine], STEP * drag, 0.0
            )

        return carry

    lax.fori_loop(0, level.shape[0], place, 0)

    basis = green[...]
    high, low = split(basis)
    green_halves[0] = high
    green_halves[1] = low
    high, low = split(basis.T)
    green_halves[2] = high
    green_halves[3] = low

    owner = info[1]
    tile = owner // 2
    lanes = lax.broadcasted_iota(jnp.int32, (8, LANES), 1) + LANES * (tile % 2)
    wave_x = jnp.where(lanes <= MID, lanes, lanes - MID).astype(F32) * (2.0 * np.pi / N)
    for part in range(4):
        ky = 8 * (tile // 2) + 4 * (owner % 2) + part
        rows = jnp.zeros((8, LANES), jnp.int32) + ky
        wave_y = jnp.where(rows <= MID, rows, rows - MID).astype(F32) * (2.0 * np.pi / N)
        square = (wave_y * wave_y + wave_x * wave_x)[0:1]
        inverse[part] = 1.0 / (eigen[...] + square)


def blend_kernel(info, partial, window, ramp, blended, keep):
    start = info[0]
    shape = pltpu.roll(ramp[...], start, 1)[0:1]
    shape = shape * info[2].astype(F32)
    lane_zero = jnp.zeros((64, LANES), F32)
    for plane in range(4):
        value = partial[plane // 2, plane % 2]
        pieces = []
        for part in range(4):
            block = window[plane * 64 : plane * 64 + 64, :]
            wide = jnp.concatenate([block, lane_zero], axis=1)
            shift = lax.rem(start - 32 * part + N, N)
            pieces.append(pltpu.roll(wide, shift, 1))
        inflow = jnp.concatenate(pieces, axis=0)
        blended[plane // 2, plane % 2] = value + shape * (inflow - value)
    keep[...] = jnp.broadcast_to(HALF * (1.0 - shape), keep.shape)


def spectrum_of(divergence, basis, basis_t):
    return times(after((basis[0], basis[1]), divergence), (basis_t[0], basis_t[1]))


def to_owners(spectrum, sent, first):
    for tile in range(64):
        r = 8 * (tile // 2)
        c = LANES * (tile % 2)
        block = spectrum[r : r + 8, c : c + LANES]
        sent[2 * tile, first : first + 4, :] = block[0:4]
        sent[2 * tile + 1, first : first + 4, :] = block[4:8]


def high_kernel(
    fields,
    partial,
    blended,
    keep,
    below_w,
    above,
    deriv,
    basis,
    basis_t,
    predicted,
    upward_low,
    ghost,
    sent,
):
    table = (deriv[0], deriv[1])
    kept = keep[0:1]
    w_low = fields[2, 0]
    w_high = fields[2, 1]
    w_ghost = below_w[0]
    u = blended[0, 1] - kept * (w_high * above[0])
    v = blended[1, 1] - kept * (w_high * above[1])
    w = partial[2, 1] - HALF * (w_high * above[2])
    low = partial[2, 0] + HALF * (w_low * w_ghost)
    predicted[0] = u
    predicted[1] = v
    predicted[2] = w
    upward_low[...] = low
    divergence = after(table, v) - times(u, table) + (w - low)
    to_owners(spectrum_of(divergence, basis, basis_t), sent, 0)
    ghost[0] = -STEP * times(w_ghost, table)
    ghost[1] = STEP * after(table, w_ghost)
    ghost[2] = low - w_ghost + HALF * (w_ghost * (w_low - below_w[1]))


def low_kernel(
    fields, blended, keep, below_uv, ghost, sent_high, deriv, basis, basis_t, predicted, sent
):
    table = (deriv[0], deriv[1])
    kept = keep[0:1]
    w_low = fields[2, 0]
    u = blended[0, 0] + kept * (w_low * below_uv[0])
    v = blended[1, 0] + kept * (w_low * below_uv[1])
    predicted[0] = u
    predicted[1] = v
    rise = ghost[2] + below_uv[0] * ghost[0] + below_uv[1] * ghost[1]
    divergence = after(table, v) - times(u, table) + rise
    sent[:, 4:8, :] = sent_high[...]
    to_owners(spectrum_of(divergence, basis, basis_t), sent, 0)


def column_kernel(modes, green_halves, inverse, out):
    gathered = jnp.concatenate([modes[pl.ds(part, N, stride=4), :] for part in range(4)], axis=1)
    scaled = after((green_halves[0], green_halves[1]), gathered)
    scaled = jnp.concatenate(
        [scaled[:, part * LANES : part * LANES + LANES] * inverse[part] for part in range(4)], axis=1
    )
    solved = after((green_halves[2], green_halves[3]), scaled)
    for part in range(4):
        out[pl.ds(part, N, stride=4), :] = solved[:, part * LANES : part * LANES + LANES]


def unpack(planes, at):
    columns = []
    for side in range(2):
        rows = []
        for block in range(32):
            tile = 2 * block + side
            rows.append(planes[2 * tile, 4 * at : 4 * at + 4, :])
            rows.append(planes[2 * tile + 1, 4 * at : 4 * at + 4, :])
        columns.append(jnp.concatenate(rows, axis=0))
    return jnp.concatenate(columns, axis=1)


def lowest_kernel(planes, basis, basis_t, lowest):
    modes = unpack(planes, 0)
    lowest[...] = times(after((basis_t[0], basis_t[1]), modes), (basis[0], basis[1]))


def correct_kernel(
    planes,
    lowest,
    predicted_low,
    upward_low,
    predicted_high,
    deriv,
    basis,
    basis_t,
    updated,
    pressure,
    upward,
):
    table = (deriv[0], deriv[1])
    low = lowest[...]
    modes = unpack(planes, 1)
    high = times(after((basis_t[0], basis_t[1]), modes), (basis[0], basis[1]))
    pressure[0, 0] = low
    pressure[0, 1] = high
    for at, value, predicted in ((0, low, predicted_low), (1, high, predicted_high)):
        updated[0, 0, at] = predicted[0] + times(value, table)
        updated[0, 1, at] = predicted[1] - after(table, value)
    updated[0, 2, 0] = upward_low[...] - (high - low)
    upward[...] = predicted_high[2] + high


def last_kernel(updated, upward, higher, result, plane, sem):
    del updated
    plane[...] = upward[...] - higher[...]
    copy = pltpu.make_async_copy(plane, result.at[0, 2, 1], sem)
    copy.start()
    copy.wait()


def call(kernel, outs, args, scalars=0, limit=24 << 20, **kwargs):
    smem = pl.BlockSpec(memory_space=pltpu.SMEM)
    vmem = pl.BlockSpec(memory_space=pltpu.VMEM)
    in_specs = [smem] * scalars + [vmem] * (len(args) - scalars)
    return pl.pallas_call(
        kernel,
        out_shape=outs,
        in_specs=in_specs,
        out_specs=jax.tree.map(lambda _: vmem, outs),
        compiler_params=pltpu.CompilerParams(vmem_limit_bytes=limit),
        **kwargs,
    )(*args)


def shaped(*dims, dtype=F32):
    return jax.ShapeDtypeStruct(dims, dtype)


def local(
    velocity,
    fringe_start,
    turbine_level,
    turbine_row,
    turbine_col,
    thrust,
    green_basis,
    eigen_shift,
):
    fields = velocity[0]
    count = lax.axis_size("gz")
    deriv = jnp.asarray(halves(derivative_table()))
    basis = jnp.asarray(halves(basis_table()))
    basis_t = jnp.asarray(halves(basis_table().T))
    ramp = jnp.asarray(ramp_row())
    slab_id = lax.axis_index("gz").astype(jnp.int32)
    group_id = lax.axis_index("group").astype(jnp.int32)
    info = jnp.concatenate([fringe_start, slab_id[None], group_id[None]])

    vmem = pl.BlockSpec(memory_space=pltpu.VMEM)
    hbm = pl.BlockSpec(memory_space=pltpu.HBM)
    up = [(i, i + 1) for i in range(count - 1)]
    down = [(i + 1, i) for i in range(count - 1)]

    rising, falling, rising_flat = pl.pallas_call(
        edges_kernel,
        out_shape=(shaped(2, N, N), shaped(3, N, N), shaped(2, N, N)),
        in_specs=[hbm],
        out_specs=(vmem, vmem, vmem),
        scratch_shapes=[pltpu.SemaphoreType.DMA((4,))],
        compiler_params=pltpu.CompilerParams(vmem_limit_bytes=8 << 20),
    )(fields)
    below_w = lax.ppermute(rising, "gz", up)
    above = lax.ppermute(falling, "gz", down)
    below_uv = lax.ppermute(rising_flat, "gz", up)
    window = call(pack_kernel, shaped(4 * 64, LANES), (info, fields), scalars=1)
    window = lax.ppermute(window, "group", [(0, 1)])

    eigen = jnp.broadcast_to(eigen_shift[:, None], (N, LANES))
    partial, green_halves, inverse = call(
        local_kernel,
        (shaped(3, 2, N, N), shaped(4, N, N, dtype=BF16), shaped(4, N, LANES)),
        (
            info,
            turbine_level,
            turbine_row,
            turbine_col,
            thrust,
            fields,
            deriv,
            green_basis,
            eigen,
        ),
        scalars=5,
    )
    blended, keep = call(
        blend_kernel,
        (shaped(2, 2, N, N), shaped(8, N)),
        (info, partial, window, ramp),
        scalars=1,
    )
    predicted_high, upward_low, ghost, sent_high = call(
        high_kernel,
        (shaped(3, N, N), shaped(N, N), shaped(3, N, N), shaped(count, 4, LANES)),
        (fields, partial, blended, keep, below_w, above, deriv, basis, basis_t),
    )
    predicted_low, sent = call(
        low_kernel,
        (shaped(2, N, N), shaped(count, 8, LANES)),
        (fields, blended, keep, below_uv, ghost, sent_high, deriv, basis, basis_t),
    )
    modes = lax.all_to_all(sent, "gz", split_axis=0, concat_axis=0, tiled=True)
    solved = call(
        column_kernel,
        shaped(count * 8, LANES),
        (modes.reshape(count * 8, LANES), green_halves, inverse),
    )
    planes = lax.all_to_all(
        solved.reshape(count, 8, LANES), "gz", split_axis=0, concat_axis=0, tiled=True
    )
    lowest = call(lowest_kernel, shaped(N, N), (planes, basis, basis_t))
    higher = lax.ppermute(lowest, "gz", down)
    updated, pressure, upward = call(
        correct_kernel,
        (shaped(1, 3, 2, N, N), shaped(1, 2, N, N), shaped(N, N)),
        (planes, lowest, predicted_low, upward_low, predicted_high, deriv, basis, basis_t),
    )
    updated = pl.pallas_call(
        last_kernel,
        out_shape=shaped(1, 3, 2, N, N),
        in_specs=[hbm, vmem, vmem],
        out_specs=hbm,
        scratch_shapes=[pltpu.VMEM((N, N), F32), pltpu.SemaphoreType.DMA],
        input_output_aliases={0: 0},
        compiler_params=pltpu.CompilerParams(vmem_limit_bytes=8 << 20),
    )(updated, upward, higher)
    return (updated, pressure)


def solution(mesh):
    return jax.shard_map(
        local,
        mesh=mesh,
        in_specs=(P("group", None, "gz", None, None), P(), P(), P(), P(), P(), P(), P()),
        out_specs=(P("group", None, "gz", None, None), P("group", "gz", None, None)),
        check_vma=False,
    )
```

```python
import numpy as np
import jax
import jax.numpy as jnp
from jax import lax
from jax.experimental import pallas as pl
from jax.experimental.pallas import tpu as pltpu
from jax.sharding import PartitionSpec as P

FRINGE = 32
N = 256
MID = N // 2
LANES = 128
STEP = 0.25
HALF = 0.5 * STEP
F32 = jnp.float32
BF16 = jnp.bfloat16


def wave_numbers():
    ids = np.arange(N)
    return np.where(ids <= MID, ids, ids - MID)


def basis_table():
    ids = np.arange(N)
    wave = wave_numbers()
    phases = 2.0 * np.pi / N * ((wave[:, None] * ids[None, :]) % N)
    edges = (ids == 0) | (ids == MID)
    norm = np.sqrt(np.where(edges, 1.0, 2.0) / N)[:, None]
    return np.where(ids[:, None] <= MID, np.cos(phases), np.sin(phases)) * norm


def derivative_table():
    basis = basis_table()
    coupling = np.zeros((N, N))
    for j in range(1, MID):
        coupling[j, j + MID] = 2.0 * np.pi * j / N
        coupling[j + MID, j] = -2.0 * np.pi * j / N
    return basis.T @ coupling @ basis


def halves(table):
    table = np.asarray(table, np.float32)
    high = table.astype(BF16)
    low = (table - high.astype(np.float32)).astype(BF16)
    return np.stack([high, low])


def ramp_row():
    offset = np.arange(FRINGE)
    row = np.zeros((8, N), np.float32)
    row[:, :FRINGE] = np.sin(np.pi * (offset + 0.5) / FRINGE) ** 2
    return row


def split(value):
    high = value.astype(BF16)
    low = (value - high.astype(F32)).astype(BF16)
    return high, low


def dot(a, b):
    return jnp.dot(a, b, preferred_element_type=F32)


def times(value, table):
    high, low = split(value)
    return dot(high, table[1]) + dot(low, table[0]) + dot(high, table[0])


def after(table, value):
    high, low = split(value)
    return dot(table[1], high) + dot(table[0], low) + dot(table[0], high)


def moved(moves, sems):
    copies = [
        pltpu.make_async_copy(source, target, sems.at[i])
        for i, (source, target) in enumerate(moves)
    ]
    for copy in copies:
        copy.start()
    for copy in copies:
        copy.wait()


def rising_kernel(fields, rising, sems):
    moved(((fields.at[:, 1], rising.at[pl.ds(0, 3)]), (fields.at[2, 0], rising.at[3])), sems)


def falling_kernel(fields, falling, sems):
    moved(((fields.at[:, 0], falling),), sems)


def pack_kernel(info, fields, window):
    start = info[0]
    lane = lax.broadcasted_iota(jnp.int32, (64, LANES), 1)
    for plane in range(4):
        packed = jnp.zeros((64, LANES), F32)
        for part in range(4):
            rows = fields[plane // 2, plane % 2, part * 64 : part * 64 + 64, :]
            shift = lax.rem(32 * part - start + N, N)
            rolled = pltpu.roll(rows, shift, 1)[:, :LANES]
            inside = (lane >= 32 * part) & (lane < 32 * part + 32)
            packed = jnp.where(inside, rolled, packed)
        window[plane * 64 : plane * 64 + 64, :] = packed


def local_kernel(
    info, level, row, col, thrust, fields, deriv, green, eigen, partial, green_halves, inverse
):
    table = (deriv[0], deriv[1])
    for at in range(2):
        u = fields[0, at]
        v = fields[1, at]
        w = fields[2, at]
        for comp in range(3):
            here = fields[comp, at]
            along_x = -times(here, table)
            along_y = after(table, here)
            other = fields[comp, 1 - at]
            vertical = w * other if at == 0 else -(w * other)
            partial[comp, at] = here - STEP * (u * along_x + v * along_y) - HALF * vertical

    is_farm = info[2]
    first_level = info[1] * 2
    lane = lax.broadcasted_iota(jnp.int32, (1, N), 1)

    def place(turbine, carry):
        at = level[turbine] - first_level

        @pl.when((at >= 0) & (at < 2) & (is_farm > 0))
        def _():
            where_row = row[turbine]
            speed = fields[0, at, pl.ds(where_row, 1), :]
            drag = -thrust[turbine] * jnp.abs(speed) * speed
            old = partial[0, at, pl.ds(where_row, 1), :]
            partial[0, at, pl.ds(where_row, 1), :] = old + jnp.where(
                lane == col[turbine], STEP * drag, 0.0
            )

        return carry

    lax.fori_loop(0, level.shape[0], place, 0)

    basis = green[...]
    high, low = split(basis)
    green_halves[0] = high
    green_halves[1] = low
    high, low = split(basis.T)
    green_halves[2] = high
    green_halves[3] = low

    owner = info[1]
    tile = owner // 2
    lanes = lax.broadcasted_iota(jnp.int32, (8, LANES), 1) + LANES * (tile % 2)
    wave_x = jnp.where(lanes <= MID, lanes, lanes - MID).astype(F32) * (2.0 * np.pi / N)
    for part in range(4):
        ky = 8 * (tile // 2) + 4 * (owner % 2) + part
        rows = jnp.zeros((8, LANES), jnp.int32) + ky
        wave_y = jnp.where(rows <= MID, rows, rows - MID).astype(F32) * (2.0 * np.pi / N)
        square = (wave_y * wave_y + wave_x * wave_x)[0:1]
        inverse[part] = 1.0 / (eigen[...] + square)


def blend_kernel(info, partial, window, ramp, blended, keep):
    start = info[0]
    shape = pltpu.roll(ramp[...], start, 1)[0:1]
    shape = shape * info[2].astype(F32)
    lane_zero = jnp.zeros((64, LANES), F32)
    for plane in range(4):
        value = partial[plane // 2, plane % 2]
        pieces = []
        for part in range(4):
            block = window[plane * 64 : plane * 64 + 64, :]
            wide = jnp.concatenate([block, lane_zero], axis=1)
            shift = lax.rem(start - 32 * part + N, N)
            pieces.append(pltpu.roll(wide, shift, 1))
        inflow = jnp.concatenate(pieces, axis=0)
        blended[plane // 2, plane % 2] = value + shape * (inflow - value)
    keep[...] = jnp.broadcast_to(HALF * (1.0 - shape), keep.shape)


def forward_kernel(
    fields, partial, blended, keep, below, above, deriv, basis, basis_t, predicted, sent
):
    table = (deriv[0], deriv[1])
    kept = keep[0:1]
    w_low = fields[2, 0]
    w_high = fields[2, 1]
    for comp in range(2):
        predicted[comp, 1] = blended[comp, 1] - kept * (w_high * above[comp])
        predicted[comp, 0] = blended[comp, 0] + kept * (w_low * below[comp])
    w_ghost = below[2]
    low = partial[2, 0] + HALF * (w_low * w_ghost)
    high = partial[2, 1] - HALF * (w_high * above[2])
    predicted[2, 0] = low
    predicted[2, 1] = high
    along_x = times(jnp.concatenate([predicted[0, 0], predicted[0, 1], w_ghost], 0), table)
    ghost = w_ghost - STEP * (below[1] * after(table, w_ghost) - below[0] * along_x[2 * N :])
    ghost = ghost - HALF * (w_ghost * (w_low - below[3]))
    div_low = after(table, predicted[1, 0]) - along_x[:N] + (low - ghost)
    div_high = after(table, predicted[1, 1]) - along_x[N : 2 * N] + (high - low)
    halfway = after((basis[0], basis[1]), jnp.concatenate([div_low, div_high], 1))
    stacked = jnp.concatenate([halfway[:, :N], halfway[:, N:]], 0)
    spectrum = times(stacked, (basis_t[0], basis_t[1]))
    for tile in range(64):
        r = 8 * (tile // 2)
        c = LANES * (tile % 2)
        lower = spectrum[r : r + 8, c : c + LANES]
        upper = spectrum[N + r : N + r + 8, c : c + LANES]
        sent[2 * tile] = jnp.concatenate([lower[0:4], upper[0:4]], 0)
        sent[2 * tile + 1] = jnp.concatenate([lower[4:8], upper[4:8]], 0)


def column_kernel(modes, green_halves, inverse, out, rows):
    gathered = jnp.concatenate([modes[pl.ds(part, N, stride=4), :] for part in range(4)], axis=1)
    scaled = after((green_halves[0], green_halves[1]), gathered)
    scaled = jnp.concatenate(
        [scaled[:, part * LANES : part * LANES + LANES] * inverse[part] for part in range(4)], axis=1
    )
    solved = after((green_halves[2], green_halves[3]), scaled)
    for part in range(4):
        rows[pl.ds(part, N, stride=4), :] = solved[:, part * LANES : part * LANES + LANES]
    slabs = N // 2
    for slab in range(slabs):
        pair = rows[8 * slab : 8 * slab + 8, :]
        out[3 * slab] = pair[0:4]
        out[3 * slab + 1] = pair[4:8]
        if slab > 0:
            out[3 * slab - 1] = pair[0:4]
    out[3 * slabs - 1] = jnp.zeros((4, LANES), F32)


def unpack(planes, at):
    columns = []
    for side in range(2):
        rows = []
        for block in range(32):
            tile = 2 * block + side
            rows.append(planes[6 * tile + at])
            rows.append(planes[6 * tile + 3 + at])
        columns.append(jnp.concatenate(rows, axis=0))
    return jnp.concatenate(columns, axis=1)


def correct_kernel(
    planes, predicted, deriv, basis, basis_t, updated, pressure, new, values, sems
):
    table = (deriv[0], deriv[1])
    modes = jnp.concatenate([unpack(planes, at) for at in range(3)], axis=1)
    halfway = after((basis_t[0], basis_t[1]), modes)
    stacked = jnp.concatenate([halfway[:, at * N : at * N + N] for at in range(3)], axis=0)
    full = times(stacked, (basis[0], basis[1]))
    copies = []

    def send(source, target):
        copy = pltpu.make_async_copy(source, target, sems.at[len(copies)])
        copy.start()
        copies.append(copy)

    for at in range(2):
        value = full[at * N : at * N + N]
        values[at] = value
        send(values.at[at], pressure.at[0, at])
        new[2, at] = predicted[2, at] - (full[at * N + N : at * N + 2 * N] - value)
        send(new.at[2, at], updated.at[0, 2, at])
    along_x = times(full[: 2 * N], table)
    for at in range(2):
        new[0, at] = predicted[0, at] + along_x[at * N : at * N + N]
        send(new.at[0, at], updated.at[0, 0, at])
    for at in range(2):
        new[1, at] = predicted[1, at] - after(table, full[at * N : at * N + N])
        send(new.at[1, at], updated.at[0, 1, at])
    for copy in copies:
        copy.wait()


def call(kernel, outs, args, scalars=0, limit=24 << 20, **kwargs):
    smem = pl.BlockSpec(memory_space=pltpu.SMEM)
    vmem = pl.BlockSpec(memory_space=pltpu.VMEM)
    in_specs = [smem] * scalars + [vmem] * (len(args) - scalars)
    return pl.pallas_call(
        kernel,
        out_shape=outs,
        in_specs=in_specs,
        out_specs=jax.tree.map(lambda _: vmem, outs),
        compiler_params=pltpu.CompilerParams(vmem_limit_bytes=limit),
        **kwargs,
    )(*args)


def shaped(*dims, dtype=F32):
    return jax.ShapeDtypeStruct(dims, dtype)


def local(
    velocity,
    fringe_start,
    turbine_level,
    turbine_row,
    turbine_col,
    thrust,
    green_basis,
    eigen_shift,
):
    fields = velocity[0]
    count = lax.axis_size("gz")
    deriv = jnp.asarray(halves(derivative_table()))
    basis = jnp.asarray(halves(basis_table()))
    basis_t = jnp.asarray(halves(basis_table().T))
    ramp = jnp.asarray(ramp_row())
    slab_id = lax.axis_index("gz").astype(jnp.int32)
    group_id = lax.axis_index("group").astype(jnp.int32)
    info = jnp.concatenate([fringe_start, slab_id[None], group_id[None]])

    vmem = pl.BlockSpec(memory_space=pltpu.VMEM)
    hbm = pl.BlockSpec(memory_space=pltpu.HBM)
    up = [(i, i + 1) for i in range(count - 1)]
    down = [(i + 1, i) for i in range(count - 1)]

    stay = pltpu.with_memory_space_constraint(fields, pltpu.HBM)

    def edges(kernel, planes):
        return pl.pallas_call(
            kernel,
            out_shape=pltpu.VMEM((planes, N, N), F32),
            in_specs=[hbm],
            out_specs=vmem,
            scratch_shapes=[pltpu.SemaphoreType.DMA((2,))],
            compiler_params=pltpu.CompilerParams(vmem_limit_bytes=8 << 20),
        )(stay)

    below = lax.ppermute(edges(rising_kernel, 4), "gz", up)
    above = lax.ppermute(edges(falling_kernel, 3), "gz", down)
    window = call(pack_kernel, shaped(4 * 64, LANES), (info, fields), scalars=1)
    window = lax.ppermute(window, "group", [(0, 1)])

    eigen = jnp.broadcast_to(eigen_shift[:, None], (N, LANES))
    partial, green_halves, inverse = call(
        local_kernel,
        (shaped(3, 2, N, N), shaped(4, N, N, dtype=BF16), shaped(4, N, LANES)),
        (
            info,
            turbine_level,
            turbine_row,
            turbine_col,
            thrust,
            fields,
            deriv,
            green_basis,
            eigen,
        ),
        scalars=5,
    )
    blended, keep = call(
        blend_kernel,
        (shaped(2, 2, N, N), shaped(8, N)),
        (info, partial, window, ramp),
        scalars=1,
    )
    predicted, sent = call(
        forward_kernel,
        (shaped(3, 2, N, N), shaped(count, 8, LANES)),
        (fields, partial, blended, keep, below, above, deriv, basis, basis_t),
    )
    modes = lax.all_to_all(sent, "gz", split_axis=0, concat_axis=0, tiled=True)
    solved = call(
        column_kernel,
        shaped(count * 3, 4, LANES),
        (modes.reshape(count * 8, LANES), green_halves, inverse),
        scratch_shapes=[pltpu.VMEM((count * 8, LANES), F32)],
    )
    planes = lax.all_to_all(solved, "gz", split_axis=0, concat_axis=0, tiled=True)
    updated, pressure = pl.pallas_call(
        correct_kernel,
        out_shape=(shaped(1, 3, 2, N, N), shaped(1, 2, N, N)),
        in_specs=[vmem] * 5,
        out_specs=(hbm, hbm),
        scratch_shapes=[
            pltpu.VMEM((3, 2, N, N), F32),
            pltpu.VMEM((2, N, N), F32),
            pltpu.SemaphoreType.DMA((8,)),
        ],
        compiler_params=pltpu.CompilerParams(vmem_limit_bytes=24 << 20),
    )(planes, predicted, deriv, basis, basis_t)
    return (updated, pressure)


def solution(mesh):
    return jax.shard_map(
        local,
        mesh=mesh,
        in_specs=(P("group", None, "gz", None, None), P(), P(), P(), P(), P(), P(), P()),
        out_specs=(P("group", None, "gz", None, None), P("group", "gz", None, None)),
        check_vma=False,
    )
```

```python
import numpy as np
import jax
import jax.numpy as jnp
from jax import lax
from jax.experimental import pallas as pl
from jax.experimental.pallas import tpu as pltpu
from jax.sharding import PartitionSpec as P

FRINGE = 32
N = 256
MID = N // 2
LANES = 128
STEP = 0.25
HALF = 0.5 * STEP
F32 = jnp.float32
BF16 = jnp.bfloat16


def wave_numbers():
    ids = np.arange(N)
    return np.where(ids <= MID, ids, ids - MID)


def basis_table():
    ids = np.arange(N)
    wave = wave_numbers()
    phases = 2.0 * np.pi / N * ((wave[:, None] * ids[None, :]) % N)
    edges = (ids == 0) | (ids == MID)
    norm = np.sqrt(np.where(edges, 1.0, 2.0) / N)[:, None]
    return np.where(ids[:, None] <= MID, np.cos(phases), np.sin(phases)) * norm


def derivative_table():
    basis = basis_table()
    coupling = np.zeros((N, N))
    for j in range(1, MID):
        coupling[j, j + MID] = 2.0 * np.pi * j / N
        coupling[j + MID, j] = -2.0 * np.pi * j / N
    return basis.T @ coupling @ basis


def halves(table):
    table = np.asarray(table, np.float32)
    high = table.astype(BF16)
    low = (table - high.astype(np.float32)).astype(BF16)
    return np.stack([high, low])


def ramp_row():
    offset = np.arange(FRINGE)
    row = np.zeros((8, N), np.float32)
    row[:, :FRINGE] = np.sin(np.pi * (offset + 0.5) / FRINGE) ** 2
    return row


def split(value):
    high = value.astype(BF16)
    low = (value - high.astype(F32)).astype(BF16)
    return high, low


def dot(a, b):
    return jnp.dot(a, b, preferred_element_type=F32)


def times(value, table):
    high, low = split(value)
    return dot(high, table[1]) + dot(low, table[0]) + dot(high, table[0])


def after(table, value):
    high, low = split(value)
    return dot(table[1], high) + dot(table[0], low) + dot(table[0], high)


def edges_kernel(start_ref, fields, rising, falling, window, sems):
    moves = (
        (fields.at[:, 1], rising.at[pl.ds(0, 3)]),
        (fields.at[:, 0], falling),
        (fields.at[2, 0], rising.at[3]),
    )
    copies = [
        pltpu.make_async_copy(source, target, sems.at[i])
        for i, (source, target) in enumerate(moves)
    ]
    for copy in copies:
        copy.start()
    start = start_ref[0]
    lane = lax.broadcasted_iota(jnp.int32, (64, LANES), 1)
    for at, planes in ((1, rising), (0, falling)):
        copies[1 - at].wait()
        for comp in range(2):
            packed = jnp.zeros((64, LANES), F32)
            for part in range(4):
                rows = planes[comp, part * 64 : part * 64 + 64, :]
                shift = lax.rem(32 * part - start + N, N)
                rolled = pltpu.roll(rows, shift, 1)[:, :LANES]
                inside = (lane >= 32 * part) & (lane < 32 * part + 32)
                packed = jnp.where(inside, rolled, packed)
            plane = comp * 2 + at
            window[plane * 64 : plane * 64 + 64, :] = packed
    copies[2].wait()


def local_kernel(
    level, row, col, thrust, fields, deriv, green, eigen, partial, green_halves, inverse
):
    table = (deriv[0], deriv[1])
    for at in range(2):
        u = fields[0, at]
        v = fields[1, at]
        w = fields[2, at]
        for comp in range(3):
            here = fields[comp, at]
            along_x = -times(here, table)
            along_y = after(table, here)
            other = fields[comp, 1 - at]
            vertical = w * other if at == 0 else -(w * other)
            partial[comp, at] = here - STEP * (u * along_x + v * along_y) - HALF * vertical

    is_farm = lax.axis_index("group")
    owner = lax.axis_index("gz")
    first_level = owner * 2
    lane = lax.broadcasted_iota(jnp.int32, (1, N), 1)

    def place(turbine, carry):
        at = level[turbine] - first_level

        @pl.when((at >= 0) & (at < 2) & (is_farm > 0))
        def _():
            where_row = row[turbine]
            speed = fields[0, at, pl.ds(where_row, 1), :]
            drag = -thrust[turbine] * jnp.abs(speed) * speed
            old = partial[0, at, pl.ds(where_row, 1), :]
            partial[0, at, pl.ds(where_row, 1), :] = old + jnp.where(
                lane == col[turbine], STEP * drag, 0.0
            )

        return carry

    lax.fori_loop(0, level.shape[0], place, 0)

    basis = green[...]
    high, low = split(basis)
    green_halves[0] = high
    green_halves[1] = low
    high, low = split(basis.T)
    green_halves[2] = high
    green_halves[3] = low

    tile = owner // 2
    lanes = lax.broadcasted_iota(jnp.int32, (8, LANES), 1) + LANES * (tile % 2)
    wave_x = jnp.where(lanes <= MID, lanes, lanes - MID).astype(F32) * (2.0 * np.pi / N)
    for part in range(4):
        ky = 8 * (tile // 2) + 4 * (owner % 2) + part
        rows = jnp.zeros((8, LANES), jnp.int32) + ky
        wave_y = jnp.where(rows <= MID, rows, rows - MID).astype(F32) * (2.0 * np.pi / N)
        square = (wave_y * wave_y + wave_x * wave_x)[0:1]
        inverse[part] = 1.0 / (eigen[...] + square)


def blend_kernel(start_ref, partial, window, ramp, blended, keep):
    start = start_ref[0]
    shape = pltpu.roll(ramp[...], start, 1)[0:1]
    shape = shape * lax.axis_index("group").astype(F32)
    lane_zero = jnp.zeros((64, LANES), F32)
    for plane in range(4):
        value = partial[plane // 2, plane % 2]
        pieces = []
        for part in range(4):
            block = window[plane * 64 : plane * 64 + 64, :]
            wide = jnp.concatenate([block, lane_zero], axis=1)
            shift = lax.rem(start - 32 * part + N, N)
            pieces.append(pltpu.roll(wide, shift, 1))
        inflow = jnp.concatenate(pieces, axis=0)
        blended[plane // 2, plane % 2] = value + shape * (inflow - value)
    keep[...] = jnp.broadcast_to(HALF * (1.0 - shape), keep.shape)


def forward_kernel(
    fields, partial, blended, keep, below, above, deriv, basis, basis_t, predicted, sent
):
    table = (deriv[0], deriv[1])
    kept = keep[0:1]
    w_low = fields[2, 0]
    w_high = fields[2, 1]
    for comp in range(2):
        predicted[comp, 1] = blended[comp, 1] - kept * (w_high * above[comp])
        predicted[comp, 0] = blended[comp, 0] + kept * (w_low * below[comp])
    w_ghost = below[2]
    low = partial[2, 0] + HALF * (w_low * w_ghost)
    high = partial[2, 1] - HALF * (w_high * above[2])
    predicted[2, 0] = low
    predicted[2, 1] = high
    along_x = times(jnp.concatenate([predicted[0, 0], predicted[0, 1], w_ghost], 0), table)
    ghost = w_ghost - STEP * (below[1] * after(table, w_ghost) - below[0] * along_x[2 * N :])
    ghost = ghost - HALF * (w_ghost * (w_low - below[3]))
    div_low = after(table, predicted[1, 0]) - along_x[:N] + (low - ghost)
    div_high = after(table, predicted[1, 1]) - along_x[N : 2 * N] + (high - low)
    halfway = after((basis[0], basis[1]), jnp.concatenate([div_low, div_high], 1))
    stacked = jnp.concatenate([halfway[:, :N], halfway[:, N:]], 0)
    spectrum = times(stacked, (basis_t[0], basis_t[1]))
    for tile in range(64):
        r = 8 * (tile // 2)
        c = LANES * (tile % 2)
        lower = spectrum[r : r + 8, c : c + LANES]
        upper = spectrum[N + r : N + r + 8, c : c + LANES]
        sent[2 * tile] = jnp.concatenate([lower[0:4], upper[0:4]], 0)
        sent[2 * tile + 1] = jnp.concatenate([lower[4:8], upper[4:8]], 0)


def column_kernel(modes, green_halves, inverse, out, rows):
    gathered = jnp.concatenate([modes[pl.ds(part, N, stride=4), :] for part in range(4)], axis=1)
    scaled = after((green_halves[0], green_halves[1]), gathered)
    scaled = jnp.concatenate(
        [scaled[:, part * LANES : part * LANES + LANES] * inverse[part] for part in range(4)], axis=1
    )
    solved = after((green_halves[2], green_halves[3]), scaled)
    for part in range(4):
        rows[pl.ds(part, N, stride=4), :] = solved[:, part * LANES : part * LANES + LANES]
    slabs = N // 2
    for slab in range(slabs):
        pair = rows[8 * slab : 8 * slab + 8, :]
        out[3 * slab] = pair[0:4]
        out[3 * slab + 1] = pair[4:8]
        if slab > 0:
            out[3 * slab - 1] = pair[0:4]
    out[3 * slabs - 1] = jnp.zeros((4, LANES), F32)


def unpack(planes, at):
    columns = []
    for side in range(2):
        rows = []
        for block in range(32):
            tile = 2 * block + side
            rows.append(planes[6 * tile + at])
            rows.append(planes[6 * tile + 3 + at])
        columns.append(jnp.concatenate(rows, axis=0))
    return jnp.concatenate(columns, axis=1)


def correct_kernel(
    planes, predicted, deriv, basis, basis_t, updated, pressure, new, values, sems
):
    table = (deriv[0], deriv[1])
    modes = jnp.concatenate([unpack(planes, at) for at in range(3)], axis=1)
    halfway = after((basis_t[0], basis_t[1]), modes)
    stacked = jnp.concatenate([halfway[:, at * N : at * N + N] for at in range(3)], axis=0)
    full = times(stacked, (basis[0], basis[1]))
    copies = []

    def send(source, target):
        copy = pltpu.make_async_copy(source, target, sems.at[len(copies)])
        copy.start()
        copies.append(copy)

    for at in range(2):
        value = full[at * N : at * N + N]
        values[at] = value
        send(values.at[at], pressure.at[0, at])
        new[2, at] = predicted[2, at] - (full[at * N + N : at * N + 2 * N] - value)
        send(new.at[2, at], updated.at[0, 2, at])
    along_x = times(full[: 2 * N], table)
    for at in range(2):
        new[0, at] = predicted[0, at] + along_x[at * N : at * N + N]
        send(new.at[0, at], updated.at[0, 0, at])
    for at in range(2):
        new[1, at] = predicted[1, at] - after(table, full[at * N : at * N + N])
        send(new.at[1, at], updated.at[0, 1, at])
    for copy in copies:
        copy.wait()


def call(kernel, outs, args, scalars=0, limit=24 << 20, **kwargs):
    smem = pl.BlockSpec(memory_space=pltpu.SMEM)
    vmem = pl.BlockSpec(memory_space=pltpu.VMEM)
    in_specs = [smem] * scalars + [vmem] * (len(args) - scalars)
    return pl.pallas_call(
        kernel,
        out_shape=outs,
        in_specs=in_specs,
        out_specs=jax.tree.map(lambda _: vmem, outs),
        compiler_params=pltpu.CompilerParams(vmem_limit_bytes=limit),
        **kwargs,
    )(*args)


def shaped(*dims, dtype=F32):
    return jax.ShapeDtypeStruct(dims, dtype)


def local(
    velocity,
    fringe_start,
    turbine_level,
    turbine_row,
    turbine_col,
    thrust,
    green_basis,
    eigen_shift,
):
    fields = velocity[0]
    count = lax.axis_size("gz")
    deriv = jnp.asarray(halves(derivative_table()))
    basis = jnp.asarray(halves(basis_table()))
    basis_t = jnp.asarray(halves(basis_table().T))
    ramp = jnp.asarray(ramp_row())
    vmem = pl.BlockSpec(memory_space=pltpu.VMEM)
    hbm = pl.BlockSpec(memory_space=pltpu.HBM)
    up = [(i, i + 1) for i in range(count - 1)]
    down = [(i + 1, i) for i in range(count - 1)]

    rising, falling, window = pl.pallas_call(
        edges_kernel,
        out_shape=(
            pltpu.VMEM((4, N, N), F32),
            pltpu.VMEM((3, N, N), F32),
            pltpu.VMEM((4 * 64, LANES), F32),
        ),
        in_specs=[pl.BlockSpec(memory_space=pltpu.SMEM), hbm],
        out_specs=(vmem, vmem, vmem),
        scratch_shapes=[pltpu.SemaphoreType.DMA((3,))],
        compiler_params=pltpu.CompilerParams(vmem_limit_bytes=8 << 20),
    )(fringe_start, pltpu.with_memory_space_constraint(fields, pltpu.HBM))
    below = lax.ppermute(rising, "gz", up)
    above = lax.ppermute(falling, "gz", down)
    window = lax.ppermute(window, "group", [(0, 1)])

    eigen = jnp.broadcast_to(eigen_shift[:, None], (N, LANES))
    partial, green_halves, inverse = call(
        local_kernel,
        (shaped(3, 2, N, N), shaped(4, N, N, dtype=BF16), shaped(4, N, LANES)),
        (
            turbine_level,
            turbine_row,
            turbine_col,
            thrust,
            fields,
            deriv,
            green_basis,
            eigen,
        ),
        scalars=4,
    )
    blended, keep = call(
        blend_kernel,
        (shaped(2, 2, N, N), shaped(8, N)),
        (fringe_start, partial, window, ramp),
        scalars=1,
    )
    predicted, sent = call(
        forward_kernel,
        (shaped(3, 2, N, N), shaped(count, 8, LANES)),
        (
            fields,
            partial,
            blended,
            keep,
            pltpu.with_memory_space_constraint(below, pltpu.VMEM),
            pltpu.with_memory_space_constraint(above, pltpu.VMEM),
            deriv,
            basis,
            basis_t,
        ),
    )
    modes = lax.all_to_all(sent, "gz", split_axis=0, concat_axis=0, tiled=True)
    solved = call(
        column_kernel,
        shaped(count * 3, 4, LANES),
        (modes.reshape(count * 8, LANES), green_halves, inverse),
        scratch_shapes=[pltpu.VMEM((count * 8, LANES), F32)],
    )
    planes = lax.all_to_all(solved, "gz", split_axis=0, concat_axis=0, tiled=True)
    updated, pressure = pl.pallas_call(
        correct_kernel,
        out_shape=(shaped(1, 3, 2, N, N), shaped(1, 2, N, N)),
        in_specs=[vmem] * 5,
        out_specs=(hbm, hbm),
        scratch_shapes=[
            pltpu.VMEM((3, 2, N, N), F32),
            pltpu.VMEM((2, N, N), F32),
            pltpu.SemaphoreType.DMA((8,)),
        ],
        compiler_params=pltpu.CompilerParams(vmem_limit_bytes=24 << 20),
    )(planes, predicted, deriv, basis, basis_t)
    return (updated, pressure)


def solution(mesh):
    return jax.shard_map(
        local,
        mesh=mesh,
        in_specs=(P("group", None, "gz", None, None), P(), P(), P(), P(), P(), P(), P()),
        out_specs=(P("group", None, "gz", None, None), P("group", "gz", None, None)),
        check_vma=False,
    )
```

```python
import numpy as np
import jax
import jax.numpy as jnp
from jax import lax
from jax.experimental import pallas as pl
from jax.experimental.pallas import tpu as pltpu
from jax.sharding import PartitionSpec as P

FRINGE = 32
N = 256
MID = N // 2
LANES = 128
STEP = 0.25
HALF = 0.5 * STEP
F32 = jnp.float32
BF16 = jnp.bfloat16


def wave_numbers():
    ids = np.arange(N)
    return np.where(ids <= MID, ids, ids - MID)


def basis_table():
    ids = np.arange(N)
    wave = wave_numbers()
    phases = 2.0 * np.pi / N * ((wave[:, None] * ids[None, :]) % N)
    edges = (ids == 0) | (ids == MID)
    norm = np.sqrt(np.where(edges, 1.0, 2.0) / N)[:, None]
    return np.where(ids[:, None] <= MID, np.cos(phases), np.sin(phases)) * norm


def derivative_table():
    basis = basis_table()
    coupling = np.zeros((N, N))
    for j in range(1, MID):
        coupling[j, j + MID] = 2.0 * np.pi * j / N
        coupling[j + MID, j] = -2.0 * np.pi * j / N
    return basis.T @ coupling @ basis


def halves(table):
    table = np.asarray(table, np.float32)
    high = table.astype(BF16)
    low = (table - high.astype(np.float32)).astype(BF16)
    return np.stack([high, low])


def ramp_row():
    offset = np.arange(FRINGE)
    row = np.zeros((8, N), np.float32)
    row[:, :FRINGE] = np.sin(np.pi * (offset + 0.5) / FRINGE) ** 2
    return row


def split(value):
    high = value.astype(BF16)
    low = (value - high.astype(F32)).astype(BF16)
    return high, low


def dot(a, b):
    return jnp.dot(a, b, preferred_element_type=F32)


def times(value, table):
    high, low = split(value)
    return dot(high, table[1]) + dot(low, table[0]) + dot(high, table[0])


def after(table, value):
    high, low = split(value)
    return dot(table[1], high) + dot(table[0], low) + dot(table[0], high)


def edge_moves(fields, edge, at, sems):
    copies = [
        pltpu.make_async_copy(fields.at[:, at], edge.at[pl.ds(0, 3)], sems.at[0]),
        pltpu.make_async_copy(fields.at[2, 1 - at], edge.at[3], sems.at[1]),
    ]
    for copy in copies:
        copy.start()
    return copies


def outer_kernel(fields, outer, sems):
    for copy in edge_moves(fields, outer, lax.rem(lax.axis_index("gz"), 2), sems):
        copy.wait()


def inner_kernel(start_ref, outer, fields, inner, window, sems):
    facing = lax.rem(lax.axis_index("gz"), 2)
    hidden = 1 - facing
    copies = edge_moves(fields, inner, hidden, sems)
    start = start_ref[0]
    lane = lax.broadcasted_iota(jnp.int32, (64, LANES), 1)
    for at, planes in ((facing, outer), (hidden, inner)):
        if planes is inner:
            for copy in copies:
                copy.wait()
        for comp in range(2):
            packed = jnp.zeros((64, LANES), F32)
            for part in range(4):
                rows = planes[comp, part * 64 : part * 64 + 64, :]
                shift = lax.rem(32 * part - start + N, N)
                rolled = pltpu.roll(rows, shift, 1)[:, :LANES]
                inside = (lane >= 32 * part) & (lane < 32 * part + 32)
                packed = jnp.where(inside, rolled, packed)
            row = pl.multiple_of((comp * 2 + at) * 64, 64)
            window[pl.ds(row, 64), :] = packed


def local_kernel(
    level,
    row,
    col,
    thrust,
    fields,
    eigen,
    tables_hbm,
    green_hbm,
    partial,
    green_halves,
    inverse,
    tables,
    green,
    sems,
):
    copies = [
        pltpu.make_async_copy(tables_hbm.at[pl.ds(0, 2)], tables.at[pl.ds(0, 2)], sems.at[0]),
        pltpu.make_async_copy(green_hbm, green, sems.at[1]),
        pltpu.make_async_copy(tables_hbm.at[pl.ds(2, 4)], tables.at[pl.ds(2, 4)], sems.at[2]),
    ]
    for copy in copies:
        copy.start()

    owner = lax.axis_index("gz")
    tile = owner // 2
    lanes = lax.broadcasted_iota(jnp.int32, (8, LANES), 1) + LANES * lax.rem(tile, 2)
    wave_x = jnp.where(lanes <= MID, lanes, lanes - MID).astype(F32) * (2.0 * np.pi / N)
    for part in range(4):
        ky = 8 * (tile // 2) + 4 * lax.rem(owner, 2) + part
        rows = jnp.zeros((8, LANES), jnp.int32) + ky
        wave_y = jnp.where(rows <= MID, rows, rows - MID).astype(F32) * (2.0 * np.pi / N)
        square = (wave_y * wave_y + wave_x * wave_x)[0:1]
        inverse[part] = 1.0 / (eigen[...] + square)

    copies[0].wait()
    table = (tables[0], tables[1])
    for at in range(2):
        u = fields[0, at]
        v = fields[1, at]
        w = fields[2, at]
        for comp in range(3):
            here = fields[comp, at]
            along_x = -times(here, table)
            along_y = after(table, here)
            other = fields[comp, 1 - at]
            vertical = w * other if at == 0 else -(w * other)
            partial[comp, at] = here - STEP * (u * along_x + v * along_y) - HALF * vertical

    is_farm = lax.axis_index("group")
    first_level = owner * 2
    lane = lax.broadcasted_iota(jnp.int32, (1, N), 1)

    def place(turbine, carry):
        at = level[turbine] - first_level

        @pl.when((at >= 0) & (at < 2) & (is_farm > 0))
        def _():
            where_row = row[turbine]
            speed = fields[0, at, pl.ds(where_row, 1), :]
            drag = -thrust[turbine] * jnp.abs(speed) * speed
            old = partial[0, at, pl.ds(where_row, 1), :]
            partial[0, at, pl.ds(where_row, 1), :] = old + jnp.where(
                lane == col[turbine], STEP * drag, 0.0
            )

        return carry

    lax.fori_loop(0, level.shape[0], place, 0)

    copies[1].wait()
    high, low = split(green[...])
    green_halves[0] = high
    green_halves[1] = low
    high, low = split(green[...].T)
    green_halves[2] = high
    green_halves[3] = low
    copies[2].wait()


def blend_kernel(start_ref, partial, window, ramp, blended, keep):
    start = start_ref[0]
    shape = pltpu.roll(ramp[...], start, 1)[0:1]
    shape = shape * lax.axis_index("group").astype(F32)
    lane_zero = jnp.zeros((64, LANES), F32)
    for plane in range(4):
        value = partial[plane // 2, plane % 2]
        pieces = []
        for part in range(4):
            block = window[plane * 64 : plane * 64 + 64, :]
            wide = jnp.concatenate([block, lane_zero], axis=1)
            shift = lax.rem(start - 32 * part + N, N)
            pieces.append(pltpu.roll(wide, shift, 1))
        inflow = jnp.concatenate(pieces, axis=0)
        blended[plane // 2, plane % 2] = value + shape * (inflow - value)
    keep[...] = jnp.broadcast_to(HALF * (1.0 - shape), keep.shape)


def forward_kernel(fields, partial, blended, keep, across, beside, tables, predicted, sent):
    table = (tables[0], tables[1])
    basis = (tables[2], tables[3])
    basis_t = (tables[4], tables[5])
    facing = lax.rem(lax.axis_index("gz"), 2)
    hidden = 1 - facing
    sign = 1.0 - 2.0 * facing.astype(F32)
    kept = keep[0:1] * sign
    w_facing = fields[2, facing]
    w_hidden = fields[2, hidden]
    for comp in range(2):
        predicted[comp, facing] = blended[comp, facing] + kept * (w_facing * across[comp])
        predicted[comp, hidden] = blended[comp, hidden] - kept * (w_hidden * beside[comp])
    half = HALF * sign
    predicted[2, facing] = partial[2, facing] + half * (w_facing * across[2])
    predicted[2, hidden] = partial[2, hidden] - half * (w_hidden * beside[2])
    low = predicted[2, 0]
    high = predicted[2, 1]
    from_across = facing == 0
    below = [jnp.where(from_across, across[i], beside[i]) for i in range(4)]
    w_low = fields[2, 0]
    w_ghost = below[2]
    along_x = times(jnp.concatenate([predicted[0, 0], predicted[0, 1], w_ghost], 0), table)
    ghost = w_ghost - STEP * (below[1] * after(table, w_ghost) - below[0] * along_x[2 * N :])
    ghost = ghost - HALF * (w_ghost * (w_low - below[3]))
    div_low = after(table, predicted[1, 0]) - along_x[:N] + (low - ghost)
    div_high = after(table, predicted[1, 1]) - along_x[N : 2 * N] + (high - low)
    halfway = after(basis, jnp.concatenate([div_low, div_high], 1))
    stacked = jnp.concatenate([halfway[:, :N], halfway[:, N:]], 0)
    spectrum = times(stacked, basis_t)
    for tile in range(64):
        r = 8 * (tile // 2)
        c = LANES * (tile % 2)
        lower = spectrum[r : r + 8, c : c + LANES]
        upper = spectrum[N + r : N + r + 8, c : c + LANES]
        sent[2 * tile] = jnp.concatenate([lower[0:4], upper[0:4]], 0)
        sent[2 * tile + 1] = jnp.concatenate([lower[4:8], upper[4:8]], 0)


def column_kernel(modes, green_halves, inverse, out, rows):
    gathered = jnp.concatenate([modes[pl.ds(part, N, stride=4), :] for part in range(4)], axis=1)
    scaled = after((green_halves[0], green_halves[1]), gathered)
    scaled = jnp.concatenate(
        [scaled[:, part * LANES : part * LANES + LANES] * inverse[part] for part in range(4)], axis=1
    )
    solved = after((green_halves[2], green_halves[3]), scaled)
    for part in range(4):
        rows[pl.ds(part, N, stride=4), :] = solved[:, part * LANES : part * LANES + LANES]
    slabs = N // 2
    for slab in range(slabs):
        pair = rows[8 * slab : 8 * slab + 8, :]
        out[3 * slab] = pair[0:4]
        out[3 * slab + 1] = pair[4:8]
        if slab > 0:
            out[3 * slab - 1] = pair[0:4]
    out[3 * slabs - 1] = jnp.zeros((4, LANES), F32)


def unpack(planes, at):
    columns = []
    for side in range(2):
        rows = []
        for block in range(32):
            tile = 2 * block + side
            rows.append(planes[6 * tile + at])
            rows.append(planes[6 * tile + 3 + at])
        columns.append(jnp.concatenate(rows, axis=0))
    return jnp.concatenate(columns, axis=1)


def correct_kernel(planes, predicted, tables, updated, pressure, new, values, sems):
    table = (tables[0], tables[1])
    basis = (tables[2], tables[3])
    basis_t = (tables[4], tables[5])
    modes = jnp.concatenate([unpack(planes, at) for at in range(3)], axis=1)
    halfway = after(basis_t, modes)
    stacked = jnp.concatenate([halfway[:, at * N : at * N + N] for at in range(3)], axis=0)
    full = times(stacked, basis)
    copies = []

    def send(source, target):
        copy = pltpu.make_async_copy(source, target, sems.at[len(copies)])
        copy.start()
        copies.append(copy)

    for at in range(2):
        value = full[at * N : at * N + N]
        values[at] = value
        send(values.at[at], pressure.at[0, at])
        new[2, at] = predicted[2, at] - (full[at * N + N : at * N + 2 * N] - value)
        send(new.at[2, at], updated.at[0, 2, at])
    along_x = times(full[: 2 * N], table)
    for at in range(2):
        new[0, at] = predicted[0, at] + along_x[at * N : at * N + N]
        send(new.at[0, at], updated.at[0, 0, at])
    for at in range(2):
        new[1, at] = predicted[1, at] - after(table, full[at * N : at * N + N])
        send(new.at[1, at], updated.at[0, 1, at])
    for copy in copies:
        copy.wait()


def call(kernel, outs, args, scalars=0, limit=24 << 20, **kwargs):
    smem = pl.BlockSpec(memory_space=pltpu.SMEM)
    vmem = pl.BlockSpec(memory_space=pltpu.VMEM)
    in_specs = [smem] * scalars + [vmem] * (len(args) - scalars)
    return pl.pallas_call(
        kernel,
        out_shape=outs,
        in_specs=in_specs,
        out_specs=jax.tree.map(lambda _: vmem, outs),
        compiler_params=pltpu.CompilerParams(vmem_limit_bytes=limit),
        **kwargs,
    )(*args)


def shaped(*dims, dtype=F32):
    return jax.ShapeDtypeStruct(dims, dtype)


def local(
    velocity,
    fringe_start,
    turbine_level,
    turbine_row,
    turbine_col,
    thrust,
    green_basis,
    eigen_shift,
):
    fields = velocity[0]
    count = lax.axis_size("gz")
    basis = basis_table()
    tables = jnp.asarray(
        np.concatenate([halves(table) for table in (derivative_table(), basis, basis.T)])
    )
    ramp = jnp.asarray(ramp_row())
    vmem = pl.BlockSpec(memory_space=pltpu.VMEM)
    hbm = pl.BlockSpec(memory_space=pltpu.HBM)
    smem = pl.BlockSpec(memory_space=pltpu.SMEM)
    even = range(0, count, 2)
    odd = range(1, count - 1, 2)
    beside_pairs = [(i, i + 1) for i in even] + [(i + 1, i) for i in even]
    across_pairs = [(i, i + 1) for i in odd] + [(i + 1, i) for i in odd]

    def in_hbm(value):
        return pltpu.with_memory_space_constraint(value, pltpu.HBM)

    def in_vmem(value):
        return pltpu.with_memory_space_constraint(value, pltpu.VMEM)

    outer = pl.pallas_call(
        outer_kernel,
        out_shape=pltpu.VMEM((4, N, N), F32),
        in_specs=[hbm],
        out_specs=vmem,
        scratch_shapes=[pltpu.SemaphoreType.DMA((2,))],
        compiler_params=pltpu.CompilerParams(vmem_limit_bytes=8 << 20),
    )(in_hbm(fields))
    across = lax.ppermute(outer, "gz", across_pairs)
    inner, window = pl.pallas_call(
        inner_kernel,
        out_shape=(pltpu.VMEM((4, N, N), F32), pltpu.VMEM((4 * 64, LANES), F32)),
        in_specs=[smem, vmem, hbm],
        out_specs=(vmem, vmem),
        scratch_shapes=[pltpu.SemaphoreType.DMA((2,))],
        compiler_params=pltpu.CompilerParams(vmem_limit_bytes=8 << 20),
    )(fringe_start, in_vmem(outer), in_hbm(fields))
    beside = lax.ppermute(inner, "gz", beside_pairs)
    window = lax.ppermute(window, "group", [(0, 1)])

    eigen = jnp.broadcast_to(eigen_shift[:, None], (N, LANES))
    partial, green_halves, inverse, tables = pl.pallas_call(
        local_kernel,
        out_shape=(
            pltpu.VMEM((3, 2, N, N), F32),
            pltpu.VMEM((4, N, N), BF16),
            pltpu.VMEM((4, N, LANES), F32),
            pltpu.VMEM((6, N, N), BF16),
        ),
        in_specs=[smem] * 4 + [vmem] * 2 + [hbm] * 2,
        out_specs=[vmem] * 4,
        scratch_shapes=[pltpu.VMEM((N, N), F32), pltpu.SemaphoreType.DMA((3,))],
        compiler_params=pltpu.CompilerParams(vmem_limit_bytes=24 << 20),
    )(
        turbine_level,
        turbine_row,
        turbine_col,
        thrust,
        in_vmem(fields),
        eigen,
        in_hbm(tables),
        in_hbm(green_basis),
    )
    blended, keep = call(
        blend_kernel,
        (shaped(2, 2, N, N), shaped(8, N)),
        (fringe_start, partial, window, ramp),
        scalars=1,
    )
    predicted, sent = call(
        forward_kernel,
        (shaped(3, 2, N, N), shaped(count, 8, LANES)),
        (in_vmem(fields), partial, blended, keep, in_vmem(across), in_vmem(beside), tables),
    )
    modes = lax.all_to_all(sent, "gz", split_axis=0, concat_axis=0, tiled=True)
    solved = call(
        column_kernel,
        shaped(count * 3, 4, LANES),
        (modes.reshape(count * 8, LANES), green_halves, inverse),
        scratch_shapes=[pltpu.VMEM((count * 8, LANES), F32)],
    )
    planes = lax.all_to_all(solved, "gz", split_axis=0, concat_axis=0, tiled=True)
    updated, pressure = pl.pallas_call(
        correct_kernel,
        out_shape=(shaped(1, 3, 2, N, N), shaped(1, 2, N, N)),
        in_specs=[vmem] * 3,
        out_specs=(hbm, hbm),
        scratch_shapes=[
            pltpu.VMEM((3, 2, N, N), F32),
            pltpu.VMEM((2, N, N), F32),
            pltpu.SemaphoreType.DMA((8,)),
        ],
        compiler_params=pltpu.CompilerParams(vmem_limit_bytes=24 << 20),
    )(planes, predicted, tables)
    return (updated, pressure)


def solution(mesh):
    return jax.shard_map(
        local,
        mesh=mesh,
        in_specs=(P("group", None, "gz", None, None), P(), P(), P(), P(), P(), P(), P()),
        out_specs=(P("group", None, "gz", None, None), P("group", "gz", None, None)),
        check_vma=False,
    )
```
